32 devices in a mesh: seq: 16 (over z, x, core), head: 2 (over y).
Axes of the slice: x: 2, y: 2, z: 4, core: 2. Of those that a mesh axis runs over, the one named last changes fastest.
Arguments:
- queries: bfloat16 [16384, 4096], P('seq', 'head'), may hold values from -90 to 90
- keys: bfloat16 [16384, 4096], P('seq', 'head'), may hold values from -50 to 50
- values: bfloat16 [16384, 4096], P('seq', 'head'), may hold values from -6 to 6
- cluster_ids: int32 [16384, 32], P('seq', 'head'), may hold values from 0 to 255, as said below
- out_weight: bfloat16 [4096, 4096], P('head', 'seq'), may hold values from -2.390625 to 2.390625
Outputs:
- mixed: bfloat16 [16384, 4096], P('seq', 'head')
The draws below stay inside these ranges and needn't reach their ends.
Inputs may be any that keep to these rules, and one draw needn't show every extreme that they name: `cluster_ids`: in every head each of the 256 clusters holds at least one token.
All inputs are finite; a program needn't handle non-finite values.
Results may differ from the reference program's by a relative error of at most 0.01.
Values may be sent and summed in bfloat16 or wider, within the bound.
A program may use at most 128 MiB of HBM per device.

```python
import jax
import jax.numpy as jnp
from jax import lax

D = 4096
HEADS = 32
HDIM = 128
CLUSTERS = 256
TOK_DEV = 1024
TOKENS = 16384
HD = 4096
N_SEQ = 16
N_HEAD = 2


def label_table(key):
    base_key = jax.random.fold_in(key, 11)
    first_key, second_key = jax.random.split(base_key)
    labels = jax.random.randint(first_key, (TOKENS, HEADS), 0, CLUSTERS, dtype=jnp.int32)
    head_keys = jax.random.split(second_key, HEADS)

    def place(head_key, column):
        chosen_rows = jax.random.permutation(head_key, TOKENS)[:CLUSTERS]
        return column.at[chosen_rows].set(jnp.arange(CLUSTERS, dtype=jnp.int32))
    return jax.vmap(place, in_axes=(0, 1), out_axes=1)(head_keys, labels)


def draw_cluster_ids(key, part):
    return label_table(key)


def draw_queries(key, part):
    labels = label_table(key)
    centre_key, jitter_key = jax.random.split(jax.random.fold_in(key, 12))
    centre = 2.0 * jnp.clip(jax.random.normal(centre_key, (HEADS, CLUSTERS, HDIM), jnp.float32), -4.0, 4.0)
    member_centre = jax.vmap(lambda table, column: table[column], in_axes=(0, 1), out_axes=1)(centre, labels)
    jitter = jnp.clip(jax.random.normal(jitter_key, (TOKENS, HEADS, HDIM), jnp.float32), -4.0, 4.0)
    query_rows = member_centre + jitter
    return query_rows.reshape(TOKENS, HEADS * HDIM).astype(jnp.bfloat16)


def draw_keys(key, part):
    row_key = jax.random.fold_in(key, 21)
    key_rows = jnp.clip(jax.random.normal(row_key, (TOKENS, HEADS, HDIM), jnp.float32), -5.0, 5.0)
    return key_rows.reshape(TOKENS, HEADS * HDIM).astype(jnp.bfloat16)


def levels(rng, dims, cuts, smallest, high):
    def one(dim, blocks):
        steps = jax.random.uniform(jax.random.fold_in(jax.random.fold_in(rng, 6), dim), (blocks,), jnp.float32, smallest / len(cuts), high / len(cuts))
        return jnp.repeat(jnp.exp(steps), dims[dim] // blocks).reshape((-1,) + (1,) * (len(dims) - dim - 1))

    loudness = one(*cuts[0])
    for cut in cuts[1:]:
        loudness = loudness * one(*cut)
    return loudness


def centred(rng, extent, scale, limit, pieces=(), held_as=jnp.bfloat16):
    entries = jax.random.normal(rng, extent, jnp.float32) * scale
    if len(pieces) > 0:
        entries = levels(rng, extent, pieces, -0.22, 0.18) * entries
    return jnp.clip(entries, min=-limit, max=limit).astype(held_as)


def setup_inputs(seed: int = 0) -> dict:
    streams_of = jax.random.split(jax.random.key(seed), 6)
    queries = draw_queries(jax.random.fold_in(streams_of[5], 71), 0)
    keys = draw_keys(jax.random.fold_in(streams_of[5], 71), 0)
    values = centred(streams_of[2], (TOKENS, HD), 1.0, 6.0, ((0, 16), (1, 2)))
    cluster_ids = draw_cluster_ids(jax.random.fold_in(streams_of[5], 71), 0)
    out_weight = centred(streams_of[4], (HD, D), 0.4, 2.390625, ((0, 2), (1, 16)))
    return dict(queries=queries, keys=keys, values=values, cluster_ids=cluster_ids, out_weight=out_weight)


def per_head(head, queries, keys, values, cluster_ids):
    first_col = (head * HDIM).astype(jnp.int32)
    labels = lax.dynamic_slice_in_dim(cluster_ids, head.astype(jnp.int32), 1, 1)[:, 0]
    query_rows = lax.dynamic_slice_in_dim(queries, first_col, HDIM, 1).astype(jnp.float32)
    key_rows = lax.dynamic_slice_in_dim(keys, first_col, HDIM, 1).astype(jnp.float32)
    value_rows = lax.dynamic_slice_in_dim(values, first_col, HDIM, 1).astype(jnp.float32)
    member = (labels[:, None] == jnp.arange(CLUSTERS, dtype=jnp.int32)[None, :]).astype(jnp.float32)
    totals = jnp.dot(member.T, query_rows, precision=lax.Precision.HIGHEST)
    counts = jnp.sum(member, axis=0)
    centre = (totals / counts[:, None]).astype(jnp.bfloat16)
    centre = lax.optimization_barrier(centre).astype(jnp.float32)
    key_blocks = key_rows.reshape(N_SEQ, TOK_DEV, HDIM)
    value_blocks = value_rows.reshape(N_SEQ, TOK_DEV, HDIM)
    scores = jnp.einsum("cd,btd->cbt", centre, key_blocks, precision=lax.Precision.HIGHEST) * (1.0 / (HDIM ** 0.5))
    block_peak = jnp.max(scores, axis=2)
    weights = jnp.exp(scores - block_peak[:, :, None]).astype(jnp.bfloat16)
    weights = lax.optimization_barrier(weights).astype(jnp.float32)
    block_mass = jnp.sum(weights, axis=2)
    block_output = jnp.einsum("cbt,btd->cbd", weights, value_blocks, precision=lax.Precision.HIGHEST)
    global_peak = jnp.max(block_peak, axis=1)
    factor = jnp.exp(block_peak - global_peak[:, None])
    output_sum = jnp.sum(factor[:, :, None] * block_output, axis=1)
    mass_sum = jnp.sum(factor * block_mass, axis=1)
    centroid_out = (output_sum / mass_sum[:, None]).astype(jnp.bfloat16)
    return jnp.take(centroid_out, labels, axis=0)


def reference(queries, keys, values, cluster_ids, out_weight):
    def one_head(head):
        return per_head(head, queries, keys, values, cluster_ids)

    attended = lax.map(one_head, jnp.arange(HEADS, dtype=jnp.int32))
    attended = jnp.transpose(attended, (1, 0, 2)).reshape(TOKENS, HEADS * HDIM)
    group_rows = (HEADS * HDIM) // N_HEAD
    summed = jnp.zeros((TOKENS, D), jnp.float32)
    for group in range(N_HEAD):
        term = jnp.dot(attended[:, group * group_rows:(group + 1) * group_rows].astype(jnp.float32),
                       out_weight[group * group_rows:(group + 1) * group_rows, :].astype(jnp.float32),
                       precision=lax.Precision.HIGHEST)
        term = lax.optimization_barrier(term.astype(jnp.bfloat16))
        summed = summed + term.astype(jnp.float32)
    return summed.astype(jnp.bfloat16)
```

```python
import functools

import jax
import jax.numpy as jnp
from jax import lax
from jax.experimental import pallas as pl
from jax.experimental.pallas import tpu as pltpu
from jax.sharding import PartitionSpec as P

HDIM = 128
CLUSTERS = 256
LANES = 128
STAT = 8
MESH = pl.DeviceIdType.MESH


def columns_of(row):
    return jnp.broadcast_to(row, (LANES, LANES)).T


def greet(seq, bits, heads_n, with_heads):
    barrier = pltpu.get_barrier_semaphore()
    for bit in range(bits):
        partner = seq + (1 << bit) * (1 - 2 * (lax.rem(seq // (1 << bit), 2)))
        pl.semaphore_signal(barrier, inc=1, device_id={"seq": partner}, device_id_type=MESH)
    others = 0
    if with_heads:
        head = lax.axis_index("head")
        for step in range(1, heads_n):
            pl.semaphore_signal(
                barrier, inc=1, device_id={"head": lax.rem(head + step, heads_n)}, device_id_type=MESH
            )
            others += 1
    pl.semaphore_wait(barrier, bits + others)


def flip(seq, bit):
    digit = lax.rem(seq // (1 << bit), 2)
    return digit, seq + (1 << bit) * (1 - 2 * digit)


def halve(seq, bits, total, acc, recvs, send_sem, recv_sem, merge):
    start = jnp.int32(0)
    starts = [start]
    for bit in range(bits):
        half = total >> (bit + 1)
        digit, partner = flip(seq, bit)
        keep = start + digit * half
        give = start + (1 - digit) * half
        copy = pltpu.make_async_remote_copy(
            src_ref=acc.at[pl.ds(give, half)],
            dst_ref=recvs[bit],
            send_sem=send_sem.at[bit],
            recv_sem=recv_sem.at[bit],
            device_id={"seq": partner},
            device_id_type=MESH,
        )
        copy.start()
        copy.wait()

        def body(i, carry, keep=keep, bit=bit):
            merge(keep + i, recvs[bit], i)
            return carry

        lax.fori_loop(0, half, body, 0)
        start = keep
        starts.append(start)
    return starts


def double(seq, bits, total, starts, views, send_sem, recv_sem):
    for bit in range(bits - 1, -1, -1):
        size = total >> (bit + 1)
        _, partner = flip(seq, bit)
        copies = []
        for number, view in enumerate(views):
            part = view.at[pl.ds(starts[bit + 1], size)]
            copies.append(
                pltpu.make_async_remote_copy(
                    src_ref=part,
                    dst_ref=part,
                    send_sem=send_sem.at[bit, number],
                    recv_sem=recv_sem.at[bit, number],
                    device_id={"seq": partner},
                    device_id_type=MESH,
                )
            )
        for copy in copies:
            copy.start()
        for copy in copies:
            copy.wait()


def centre_kernel(n, bits, heads_n, rows, part_ref, ids_ref, out_ref, ids_out_ref, *scratch):
    acc, ids_all, full = scratch[:3]
    recvs = scratch[3 : 3 + bits]
    send_sem, recv_sem, gsend, grecv, isend, irecv, local_sem = scratch[3 + bits :]
    seq = lax.axis_index("seq")
    head = lax.axis_index("head")
    load = pltpu.make_async_copy(part_ref, acc, local_sem.at[0])
    load.start()
    own = pltpu.make_async_copy(ids_ref, ids_all.at[head], local_sem.at[1])
    own.start()
    greet(seq, bits, heads_n, True)
    id_copies = []
    for step in range(1, heads_n):
        copy = pltpu.make_async_remote_copy(
            src_ref=ids_ref,
            dst_ref=ids_all.at[head],
            send_sem=isend.at[step - 1],
            recv_sem=irecv.at[step - 1],
            device_id={"head": lax.rem(head + step, heads_n)},
            device_id_type=MESH,
        )
        copy.start()
        id_copies.append(copy)
    load.wait()

    def merge(chunk, recv, i):
        acc[chunk] = acc[chunk] + recv[i]

    starts = halve(seq, bits, n, acc, recvs, send_sem, recv_sem, merge)
    mine = starts[-1]
    block = min(rows, LANES)
    for b in range(rows // block):
        count = columns_of(acc[mine, rows + b : rows + b + 1, :])[:block]
        full[mine, b * block : (b + 1) * block, :] = (
            acc[mine, b * block : (b + 1) * block, :] / count
        ).astype(jnp.bfloat16)
    double(seq, bits, n, starts, [full], gsend, grecv)
    out_ref[...] = full[...]
    own.wait()
    for copy in id_copies:
        copy.wait()
    ids_out_ref[...] = ids_all[...]


def output_kernel(n, bits, heads_n, rows, part_ref, out_ref, *scratch):
    acc, full = scratch[:2]
    recvs = scratch[2 : 2 + bits]
    send_sem, recv_sem, gsend, grecv, hsend, hrecv, local_sem = scratch[2 + bits :]
    seq = lax.axis_index("seq")
    head = lax.axis_index("head")
    load = pltpu.make_async_copy(part_ref, acc, local_sem.at[0])
    load.start()
    greet(seq, bits, heads_n, True)
    load.wait()
    block = min(rows, LANES)

    def merge(chunk, recv, i):
        mine = acc[chunk, rows : rows + STAT, :]
        other = recv[i, rows : rows + STAT, :]
        for b in range(rows // block):
            peak_a, peak_b = mine[b : b + 1], other[b : b + 1]
            peak = jnp.maximum(peak_a, peak_b)
            scale_a, scale_b = jnp.exp(peak_a - peak), jnp.exp(peak_b - peak)
            acc[chunk, rows + b : rows + b + 1, :] = peak
            acc[chunk, rows + 4 + b : rows + 5 + b, :] = (
                scale_a * mine[4 + b : 5 + b] + scale_b * other[4 + b : 5 + b]
            )
            span = slice(b * block, (b + 1) * block)
            acc[chunk, span, :] = (
                acc[chunk, span, :] * columns_of(scale_a)[:block]
                + recv[i, span, :] * columns_of(scale_b)[:block]
            )

    starts = halve(seq, bits, n, acc, recvs, send_sem, recv_sem, merge)
    mine = starts[-1]
    for b in range(rows // block):
        mass = columns_of(acc[mine, rows + 4 + b : rows + 5 + b, :])[:block]
        full[head, mine, b * block : (b + 1) * block, :] = (
            acc[mine, b * block : (b + 1) * block, :] / mass
        ).astype(jnp.bfloat16)
    copies = []
    for step in range(1, heads_n):
        part = full.at[head, mine]
        copies.append(
            pltpu.make_async_remote_copy(
                src_ref=part,
                dst_ref=part,
                send_sem=hsend.at[step - 1],
                recv_sem=hrecv.at[step - 1],
                device_id={"head": lax.rem(head + step, heads_n)},
                device_id_type=MESH,
            )
        )
    for copy in copies:
        copy.start()
    for copy in copies:
        copy.wait()
    double(seq, bits, n, starts, [full.at[h] for h in range(heads_n)], gsend, grecv)
    out_ref[...] = full[...]


def local(queries, keys, values, cluster_ids, out_weight):
    n = lax.axis_size("seq")
    heads_n = lax.axis_size("head")
    bits = n.bit_length() - 1
    token_rows = queries.shape[0]
    head_count = queries.shape[1] // HDIM
    rows = head_count * CLUSTERS // n
    blocks = max(rows // LANES, 1)
    query_three = queries.reshape(token_rows, head_count, HDIM)
    key_three = keys.reshape(token_rows, head_count, HDIM)
    value_three = values.reshape(token_rows, head_count, HDIM)
    labels = jnp.arange(CLUSTERS, dtype=jnp.int32)

    low = n // heads_n
    wide = lax.all_gather(
        out_weight, "seq", axis=0, axis_index_groups=[[g * low + r for g in range(heads_n)] for r in range(low)]
    )
    tall = lax.all_to_all(wide, "head", split_axis=0, concat_axis=0, tiled=True)
    tall = tall.reshape(-1, out_weight.shape[1])
    column_weight = lax.all_gather(
        tall, "seq", axis=1, tiled=True,
        axis_index_groups=[[g * low + r for r in range(low)] for g in range(heads_n)],
    )

    ids_t = cluster_ids.T
    member = (ids_t[:, None, :] == labels[None, :, None]).astype(jnp.bfloat16)
    totals = jnp.einsum("hct,thd->hcd", member, query_three, preferred_element_type=jnp.float32)
    counts = jnp.sum(member, axis=2, dtype=jnp.float32)

    def lanes(stat):
        stat = stat.reshape(n, blocks, rows // blocks)
        return jnp.pad(stat, ((0, 0), (0, 0), (0, LANES - rows // blocks)))

    def stats(arrays):
        each = STAT // len(arrays)
        return jnp.concatenate(
            [jnp.pad(lanes(a), ((0, 0), (0, each - blocks), (0, 0))) for a in arrays], axis=1
        )

    def packed(big, arrays):
        return jnp.concatenate([big.reshape(n, rows, HDIM), stats(arrays)], axis=1)

    vmem = pl.BlockSpec(memory_space=pltpu.VMEM)
    anywhere = pl.BlockSpec(memory_space=pl.ANY)
    dma = pltpu.SemaphoreType.DMA
    recvs = [pltpu.VMEM((n >> (bit + 1), rows + STAT, LANES), jnp.float32) for bit in range(bits)]
    others = max(heads_n - 1, 1)
    centre, ids_every = pl.pallas_call(
        functools.partial(centre_kernel, n, bits, heads_n, rows),
        out_shape=(
            jax.ShapeDtypeStruct((n, rows, HDIM), jnp.bfloat16),
            jax.ShapeDtypeStruct((heads_n, head_count, token_rows), jnp.int32),
        ),
        in_specs=[anywhere, vmem],
        out_specs=(vmem, vmem),
        scratch_shapes=[
            pltpu.VMEM((n, rows + STAT, LANES), jnp.float32),
            pltpu.VMEM((heads_n, head_count, token_rows), jnp.int32),
            pltpu.VMEM((n, rows, HDIM), jnp.bfloat16),
            *recvs,
            dma((bits,)), dma((bits,)), dma((bits, 1)), dma((bits, 1)),
            dma((others,)), dma((others,)), dma((2,)),
        ],
        compiler_params=pltpu.CompilerParams(collective_id=0, has_side_effects=True),
    )(packed(totals, [counts]), ids_t)
    centre = centre.reshape(head_count, CLUSTERS, HDIM)

    scores = jnp.einsum("hcd,thd->hct", centre, key_three, preferred_element_type=jnp.float32)
    scores = scores * (1.0 / HDIM**0.5)
    block_peak = jnp.max(scores, axis=2)
    weights = jnp.exp(scores - block_peak[:, :, None]).astype(jnp.bfloat16)
    block_mass = jnp.sum(weights, axis=2, dtype=jnp.float32)
    block_output = jnp.einsum(
        "hct,thd->hcd", weights, value_three, preferred_element_type=jnp.float32
    )

    centre_every = pl.pallas_call(
        functools.partial(output_kernel, n, bits, heads_n, rows),
        out_shape=jax.ShapeDtypeStruct((heads_n, n, rows, HDIM), jnp.bfloat16),
        in_specs=[anywhere],
        out_specs=vmem,
        scratch_shapes=[
            pltpu.VMEM((n, rows + STAT, LANES), jnp.float32),
            pltpu.VMEM((heads_n, n, rows, HDIM), jnp.bfloat16),
            *recvs,
            dma((bits,)), dma((bits,)), dma((bits, heads_n)), dma((bits, heads_n)),
            dma((others,)), dma((others,)), dma((1,)),
        ],
        compiler_params=pltpu.CompilerParams(collective_id=1, has_side_effects=True),
    )(packed(block_output, [block_peak, block_mass]))
    centre_every = centre_every.reshape(heads_n * head_count, CLUSTERS, HDIM)

    ids_every = ids_every.reshape(heads_n * head_count, token_rows)
    member_every = (ids_every[:, None, :] == labels[None, :, None]).astype(jnp.bfloat16)
    attended_all = jnp.einsum(
        "hct,hcd->thd", member_every, centre_every, preferred_element_type=jnp.float32
    )
    attended_all = attended_all.astype(jnp.bfloat16).reshape(token_rows, -1)
    group_rows = attended_all.shape[1] // heads_n
    summed = jnp.zeros((token_rows, column_weight.shape[1]), jnp.float32)
    for group in range(heads_n):
        term = jnp.dot(
            attended_all[:, group * group_rows : (group + 1) * group_rows],
            column_weight[group * group_rows : (group + 1) * group_rows, :],
            preferred_element_type=jnp.float32,
        )
        summed = summed + term.astype(jnp.bfloat16).astype(jnp.float32)
    return summed.astype(jnp.bfloat16)


def solution(mesh):
    return jax.shard_map(
        local,
        mesh=mesh,
        in_specs=(
            P("seq", "head"),
            P("seq", "head"),
            P("seq", "head"),
            P("seq", "head"),
            P("head", "seq"),
        ),
        out_specs=P("seq", "head"),
        check_vma=False,
    )
```

```python
import functools

import jax
import jax.numpy as jnp
from jax import lax
from jax.experimental import pallas as pl
from jax.experimental.pallas import tpu as pltpu
from jax.sharding import PartitionSpec as P

HDIM = 128
CLUSTERS = 256
LANES = 128
STAT = 8
MESH = pl.DeviceIdType.MESH


def columns_of(row):
    return jnp.broadcast_to(row, (LANES, LANES)).T


def flip(seq, bit):
    digit = lax.rem(seq // (1 << bit), 2)
    return digit, seq + (1 << bit) * (1 - 2 * digit)


def orders_of(bits):
    straight = list(range(bits))
    return [straight, straight[:1] + straight[2:] + straight[1:2]]


def greet(seq, bits, heads_n, digits):
    barrier = pltpu.get_barrier_semaphore()
    head = lax.axis_index("head")
    n = 1 << bits
    targets = [{"seq": flip(seq, bit)[1]} for bit in range(bits)]
    targets += [{"head": lax.rem(head + step, heads_n)} for step in range(1, heads_n)]
    if digits:
        low = n // heads_n
        targets += [{"seq": lax.rem(seq + step * low, n)} for step in range(1, heads_n)]
    for target in targets:
        pl.semaphore_signal(barrier, inc=1, device_id=target, device_id_type=MESH)
    pl.semaphore_wait(barrier, len(targets))


def halve(seq, bits, acc, recvs, send_sem, recv_sem, merge):
    n = 1 << bits
    orders = orders_of(bits)
    starts = [[jnp.int32(0)] for _ in orders]

    def begin(stream, step):
        half = n >> (step + 1)
        digit, partner = flip(seq, orders[stream][step])
        start = starts[stream][step]
        give = start + (1 - digit) * half
        starts[stream].append(start + digit * half)
        copy = pltpu.make_async_remote_copy(
            src_ref=acc.at[stream, pl.ds(give, half)],
            dst_ref=recvs[step].at[stream],
            send_sem=send_sem.at[stream, step],
            recv_sem=recv_sem.at[stream, step],
            device_id={"seq": partner},
            device_id_type=MESH,
        )
        copy.start()
        return copy

    pending = [begin(stream, 0) for stream in range(len(orders))]
    for step in range(bits):
        for stream in range(len(orders)):
            pending[stream].wait()
            keep = starts[stream][step + 1]

            def body(i, carry, stream=stream, keep=keep, step=step):
                merge(stream, keep + i, recvs[step], i)
                return carry

            lax.fori_loop(0, n >> (step + 1), body, 0)
            if step + 1 < bits:
                pending[stream] = begin(stream, step + 1)
    return starts


def double(seq, bits, starts, views, send_sem, recv_sem):
    n = 1 << bits
    orders = orders_of(bits)

    def begin(stream, step):
        _, partner = flip(seq, orders[stream][step])
        copies = []
        for number, view in enumerate(views):
            part = view.at[stream, pl.ds(starts[stream][step + 1], n >> (step + 1))]
            copies.append(
                pltpu.make_async_remote_copy(
                    src_ref=part,
                    dst_ref=part,
                    send_sem=send_sem.at[stream, step, number],
                    recv_sem=recv_sem.at[stream, step, number],
                    device_id={"seq": partner},
                    device_id_type=MESH,
                )
            )
        for copy in copies:
            copy.start()
        return copies

    pending = [begin(stream, bits - 1) for stream in range(len(orders))]
    for step in range(bits - 1, -1, -1):
        for stream in range(len(orders)):
            for copy in pending[stream]:
                copy.wait()
            if step > 0:
                pending[stream] = begin(stream, step - 1)


def centre_kernel(
    bits, heads_n, rows, part_ref, ids_ref, weight_ref, out_ref, ids_out_ref, tall_ref, *scratch
):
    acc, ids_all, full, wide, tall = scratch[:5]
    recvs = scratch[5 : 5 + bits]
    send_sem, recv_sem, gsend, grecv, isend, irecv, zsend, zrecv, ysend, yrecv, local_sem, put_sem = scratch[
        5 + bits :
    ]
    seq = lax.axis_index("seq")
    head = lax.axis_index("head")
    n = 1 << bits
    low = n // heads_n
    group = seq // low
    load = pltpu.make_async_copy(part_ref, acc, local_sem.at[0])
    load.start()
    own = pltpu.make_async_copy(ids_ref, ids_all.at[head], local_sem.at[1])
    own.start()
    own_weight = pltpu.make_async_copy(weight_ref, wide.at[group], local_sem.at[2])
    own_weight.start()
    greet(seq, bits, heads_n, True)

    def to_head(step, src, dst, sends, receives):
        return pltpu.make_async_remote_copy(
            src_ref=src,
            dst_ref=dst,
            send_sem=sends.at[step - 1],
            recv_sem=receives.at[step - 1],
            device_id={"head": lax.rem(head + step, heads_n)},
            device_id_type=MESH,
        )

    load.wait()
    across = []
    for step in range(1, heads_n):
        across.append(
            pltpu.make_async_remote_copy(
                src_ref=weight_ref,
                dst_ref=wide.at[group],
                send_sem=zsend.at[step - 1],
                recv_sem=zrecv.at[step - 1],
                device_id={"seq": lax.rem(seq + step * low, n)},
                device_id_type=MESH,
            )
        )
    id_copies = [to_head(step, ids_ref, ids_all.at[head], isend, irecv) for step in range(1, heads_n)]
    for copy in across + id_copies:
        copy.start()

    def merge(stream, chunk, recv, i):
        acc[stream, chunk] = acc[stream, chunk] + recv[stream, i]

    starts = halve(seq, bits, acc, recvs, send_sem, recv_sem, merge)
    block = min(rows, LANES)
    for stream in range(2):
        mine = starts[stream][-1]
        for b in range(rows // block):
            span = slice(b * block, (b + 1) * block)
            count = columns_of(acc[stream, mine, rows + b : rows + b + 1, :])[:block]
            full[stream, mine, span, :] = (acc[stream, mine, span, :] / count).astype(jnp.bfloat16)
    own_weight.wait()
    for copy in across:
        copy.wait()
    beside = [to_head(s, wide.at[lax.rem(head + s, heads_n)], tall.at[head], ysend, yrecv) for s in range(1, heads_n)]
    for copy in beside:
        copy.start()
    puts = [pltpu.make_async_copy(wide.at[head], tall_ref.at[head], put_sem.at[0])]
    puts[0].start()
    double(seq, bits, starts, [full], gsend, grecv)
    out_ref[...] = full[...]
    own.wait()
    for copy in id_copies:
        copy.wait()
    ids_out_ref[...] = ids_all[...]
    for copy in beside:
        copy.wait()
    for step in range(1, heads_n):
        other = lax.rem(head + step, heads_n)
        puts.append(pltpu.make_async_copy(tall.at[other], tall_ref.at[other], put_sem.at[step]))
        puts[-1].start()
    for put in puts:
        put.wait()


def output_kernel(bits, heads_n, rows, part_ref, out_ref, *scratch):
    acc, full = scratch[:2]
    recvs = scratch[2 : 2 + bits]
    send_sem, recv_sem, gsend, grecv, hsend, hrecv, local_sem = scratch[2 + bits :]
    seq = lax.axis_index("seq")
    head = lax.axis_index("head")
    load = pltpu.make_async_copy(part_ref, acc, local_sem.at[0])
    load.start()
    greet(seq, bits, heads_n, False)
    load.wait()
    block = min(rows, LANES)

    def merge(stream, chunk, recv, i):
        mine = acc[stream, chunk, rows : rows + STAT, :]
        other = recv[stream, i, rows : rows + STAT, :]
        for b in range(rows // block):
            peak_a, peak_b = mine[b : b + 1], other[b : b + 1]
            peak = jnp.maximum(peak_a, peak_b)
            scale_a, scale_b = jnp.exp(peak_a - peak), jnp.exp(peak_b - peak)
            acc[stream, chunk, rows + b : rows + b + 1, :] = peak
            acc[stream, chunk, rows + 4 + b : rows + 5 + b, :] = (
                scale_a * mine[4 + b : 5 + b] + scale_b * other[4 + b : 5 + b]
            )
            span = slice(b * block, (b + 1) * block)
            acc[stream, chunk, span, :] = (
                acc[stream, chunk, span, :] * columns_of(scale_a)[:block]
                + recv[stream, i, span, :] * columns_of(scale_b)[:block]
            )

    starts = halve(seq, bits, acc, recvs, send_sem, recv_sem, merge)
    copies = []
    for stream in range(2):
        mine = starts[stream][-1]
        for b in range(rows // block):
            span = slice(b * block, (b + 1) * block)
            mass = columns_of(acc[stream, mine, rows + 4 + b : rows + 5 + b, :])[:block]
            full[head, stream, mine, span, :] = (acc[stream, mine, span, :] / mass).astype(jnp.bfloat16)
        part = full.at[head, stream, mine]
        for step in range(1, heads_n):
            copies.append(
                pltpu.make_async_remote_copy(
                    src_ref=part,
                    dst_ref=part,
                    send_sem=hsend.at[stream, step - 1],
                    recv_sem=hrecv.at[stream, step - 1],
                    device_id={"head": lax.rem(head + step, heads_n)},
                    device_id_type=MESH,
                )
            )
    for copy in copies:
        copy.start()
    for copy in copies:
        copy.wait()
    double(seq, bits, starts, [full.at[h] for h in range(heads_n)], gsend, grecv)
    out_ref[...] = full[...]


def local(queries, keys, values, cluster_ids, out_weight):
    n = lax.axis_size("seq")
    heads_n = lax.axis_size("head")
    bits = n.bit_length() - 1
    token_rows = queries.shape[0]
    head_count = queries.shape[1] // HDIM
    rows = head_count * CLUSTERS // n // 2
    blocks = max(rows // LANES, 1)
    query_three = queries.reshape(token_rows, head_count, HDIM)
    key_three = keys.reshape(token_rows, head_count, HDIM)
    value_three = values.reshape(token_rows, head_count, HDIM)
    labels = jnp.arange(CLUSTERS, dtype=jnp.int32)

    ids_t = cluster_ids.T
    member = (ids_t[:, None, :] == labels[None, :, None]).astype(jnp.bfloat16)
    totals = jnp.einsum("hct,thd->hcd", member, query_three, preferred_element_type=jnp.float32)
    counts = jnp.sum(member, axis=2, dtype=jnp.float32)

    def lanes(stat):
        stat = stat.reshape(2, n, blocks, rows // blocks)
        return jnp.pad(stat, ((0, 0), (0, 0), (0, 0), (0, LANES - rows // blocks)))

    def stats(arrays):
        each = STAT // len(arrays)
        return jnp.concatenate(
            [jnp.pad(lanes(a), ((0, 0), (0, 0), (0, each - blocks), (0, 0))) for a in arrays], axis=2
        )

    def packed(big, arrays):
        return jnp.concatenate([big.reshape(2, n, rows, HDIM), stats(arrays)], axis=2)

    vmem = pl.BlockSpec(memory_space=pltpu.VMEM)
    anywhere = pl.BlockSpec(memory_space=pl.ANY)
    dma = pltpu.SemaphoreType.DMA
    recvs = [pltpu.VMEM((2, n >> (bit + 1), rows + STAT, LANES), jnp.float32) for bit in range(bits)]
    others = max(heads_n - 1, 1)
    centre, ids_every, tall = pl.pallas_call(
        functools.partial(centre_kernel, bits, heads_n, rows),
        out_shape=(
            jax.ShapeDtypeStruct((2, n, rows, HDIM), jnp.bfloat16),
            jax.ShapeDtypeStruct((heads_n, head_count, token_rows), jnp.int32),
            jax.ShapeDtypeStruct((heads_n, *out_weight.shape), jnp.bfloat16),
        ),
        in_specs=[anywhere, vmem, anywhere],
        out_specs=(vmem, vmem, anywhere),
        scratch_shapes=[
            pltpu.VMEM((2, n, rows + STAT, LANES), jnp.float32),
            pltpu.VMEM((heads_n, head_count, token_rows), jnp.int32),
            pltpu.VMEM((2, n, rows, HDIM), jnp.bfloat16),
            pltpu.VMEM((heads_n, *out_weight.shape), jnp.bfloat16),
            pltpu.VMEM((heads_n, *out_weight.shape), jnp.bfloat16),
            *recvs,
            dma((2, bits)), dma((2, bits)), dma((2, bits, 1)), dma((2, bits, 1)),
            dma((others,)), dma((others,)), dma((others,)), dma((others,)), dma((others,)), dma((others,)),
            dma((3,)), dma((heads_n,)),
        ],
        compiler_params=pltpu.CompilerParams(collective_id=0, has_side_effects=True),
    )(packed(totals, [counts]), ids_t, out_weight)
    low = n // heads_n
    column_weight = lax.all_gather(
        tall.reshape(-1, out_weight.shape[1]), "seq", axis=1, tiled=True,
        axis_index_groups=[[g * low + r for r in range(low)] for g in range(heads_n)],
    )
    centre = centre.reshape(head_count, CLUSTERS, HDIM)

    scores = jnp.einsum("hcd,thd->hct", centre, key_three, preferred_element_type=jnp.float32)
    scores = scores * (1.0 / HDIM**0.5)
    block_peak = jnp.max(scores, axis=2)
    weights = jnp.exp(scores - block_peak[:, :, None]).astype(jnp.bfloat16)
    block_mass = jnp.sum(weights, axis=2, dtype=jnp.float32)
    block_output = jnp.einsum(
        "hct,thd->hcd", weights, value_three, preferred_element_type=jnp.float32
    )

    centre_every = pl.pallas_call(
        functools.partial(output_kernel, bits, heads_n, rows),
        out_shape=jax.ShapeDtypeStruct((heads_n, 2, n, rows, HDIM), jnp.bfloat16),
        in_specs=[anywhere],
        out_specs=vmem,
        scratch_shapes=[
            pltpu.VMEM((2, n, rows + STAT, LANES), jnp.float32),
            pltpu.VMEM((heads_n, 2, n, rows, HDIM), jnp.bfloat16),
            *recvs,
            dma((2, bits)), dma((2, bits)), dma((2, bits, heads_n)), dma((2, bits, heads_n)),
            dma((2, others)), dma((2, others)), dma((1,)),
        ],
        compiler_params=pltpu.CompilerParams(collective_id=1, has_side_effects=True),
    )(packed(block_output, [block_peak, block_mass]))
    centre_every = centre_every.reshape(heads_n * head_count, CLUSTERS, HDIM)

    ids_every = ids_every.reshape(heads_n * head_count, token_rows)
    member_every = (ids_every[:, None, :] == labels[None, :, None]).astype(jnp.bfloat16)
    attended_all = jnp.einsum(
        "hct,hcd->thd", member_every, centre_every, preferred_element_type=jnp.float32
    )
    attended_all = attended_all.astype(jnp.bfloat16).reshape(token_rows, -1)
    group_rows = attended_all.shape[1] // heads_n
    summed = jnp.zeros((token_rows, column_weight.shape[1]), jnp.float32)
    for group in range(heads_n):
        term = jnp.dot(
            attended_all[:, group * group_rows : (group + 1) * group_rows],
            column_weight[group * group_rows : (group + 1) * group_rows, :],
            preferred_element_type=jnp.float32,
        )
        summed = summed + term.astype(jnp.bfloat16).astype(jnp.float32)
    return summed.astype(jnp.bfloat16)


def solution(mesh):
    return jax.shard_map(
        local,
        mesh=mesh,
        in_specs=(
            P("seq", "head"),
            P("seq", "head"),
            P("seq", "head"),
            P("seq", "head"),
            P("head", "seq"),
        ),
        out_specs=P("seq", "head"),
        check_vma=False,
    )
```

```python
import functools

import jax
import jax.numpy as jnp
from jax import lax
from jax.experimental import pallas as pl
from jax.experimental.pallas import tpu as pltpu
from jax.sharding import PartitionSpec as P

HDIM = 128
CLUSTERS = 256
LANES = 128
STAT = 8
PIECES = 4
MESH = pl.DeviceIdType.MESH


def columns_of(row):
    return jnp.broadcast_to(row, (LANES, LANES)).T


def flip(seq, bit):
    digit = lax.rem(seq // (1 << bit), 2)
    return digit, seq + (1 << bit) * (1 - 2 * digit)


def orders_of(bits):
    straight = list(range(bits))
    return [straight, straight[:1] + straight[2:] + straight[1:2]]


def greet(seq, bits, heads_n, digits):
    barrier = pltpu.get_barrier_semaphore()
    head = lax.axis_index("head")
    n = 1 << bits
    targets = [{"seq": flip(seq, bit)[1]} for bit in range(bits)]
    targets += [{"head": lax.rem(head + step, heads_n)} for step in range(1, heads_n)]
    if digits:
        low = n // heads_n
        targets += [{"seq": lax.rem(seq + step * low, n)} for step in range(1, heads_n)]
    for target in targets:
        pl.semaphore_signal(barrier, inc=1, device_id=target, device_id_type=MESH)
    pl.semaphore_wait(barrier, len(targets))


def halve(seq, bits, acc, recvs, send_sem, recv_sem, merge, beside=None):
    n = 1 << bits
    orders = orders_of(bits)
    starts = [[jnp.int32(0)] for _ in orders]

    def begin(stream, step):
        half = n >> (step + 1)
        digit, partner = flip(seq, orders[stream][step])
        start = starts[stream][step]
        give = start + (1 - digit) * half
        starts[stream].append(start + digit * half)
        copy = pltpu.make_async_remote_copy(
            src_ref=acc.at[stream, pl.ds(give, half)],
            dst_ref=recvs[step].at[stream],
            send_sem=send_sem.at[stream, step],
            recv_sem=recv_sem.at[stream, step],
            device_id={"seq": partner},
            device_id_type=MESH,
        )
        copy.start()
        return copy

    pending = [begin(stream, 0) for stream in range(len(orders))]
    for step in range(bits):
        for stream in range(len(orders)):
            pending[stream].wait()
            keep = starts[stream][step + 1]

            def body(i, carry, stream=stream, keep=keep, step=step):
                merge(stream, keep + i, recvs[step], i)
                return carry

            lax.fori_loop(0, n >> (step + 1), body, 0)
            if step + 1 < bits:
                pending[stream] = begin(stream, step + 1)
        if beside is not None:
            beside(step)
    return starts


def double(seq, bits, starts, views, send_sem, recv_sem, beside=None):
    n = 1 << bits
    orders = orders_of(bits)

    def begin(stream, step):
        _, partner = flip(seq, orders[stream][step])
        copies = []
        for number, view in enumerate(views):
            part = view.at[stream, pl.ds(starts[stream][step + 1], n >> (step + 1))]
            copies.append(
                pltpu.make_async_remote_copy(
                    src_ref=part,
                    dst_ref=part,
                    send_sem=send_sem.at[stream, step, number],
                    recv_sem=recv_sem.at[stream, step, number],
                    device_id={"seq": partner},
                    device_id_type=MESH,
                )
            )
        for copy in copies:
            copy.start()
        return copies

    pending = [begin(stream, bits - 1) for stream in range(len(orders))]
    for step in range(bits - 1, -1, -1):
        for stream in range(len(orders)):
            for copy in pending[stream]:
                copy.wait()
            if step > 0:
                pending[stream] = begin(stream, step - 1)
        if beside is not None and step > 0:
            beside(2 * bits - 1 - step)


def centre_kernel(
    bits, heads_n, rows, part_ref, ids_ref, weight_ref, out_ref, ids_out_ref, tall_ref, *scratch
):
    acc, ids_all, full, wide, tall = scratch[:5]
    recvs = scratch[5 : 5 + bits]
    send_sem, recv_sem, gsend, grecv, isend, irecv, zsend, zrecv, ysend, yrecv, local_sem, put_sem = scratch[
        5 + bits :
    ]
    seq = lax.axis_index("seq")
    head = lax.axis_index("head")
    n = 1 << bits
    low = n // heads_n
    group = seq // low
    load = pltpu.make_async_copy(part_ref, acc, local_sem.at[0])
    load.start()
    own = pltpu.make_async_copy(ids_ref, ids_all.at[head], local_sem.at[1])
    own.start()
    own_weight = pltpu.make_async_copy(weight_ref, wide.at[group], local_sem.at[2])
    own_weight.start()
    greet(seq, bits, heads_n, True)

    def to_head(step, src, dst, sends, receives):
        return pltpu.make_async_remote_copy(
            src_ref=src,
            dst_ref=dst,
            send_sem=sends(step - 1),
            recv_sem=receives(step - 1),
            device_id={"head": lax.rem(head + step, heads_n)},
            device_id_type=MESH,
        )

    height = weight_ref.shape[0] // PIECES

    def across(piece):
        span = pl.ds(piece * height, height)
        return [
            pltpu.make_async_remote_copy(
                src_ref=weight_ref.at[span],
                dst_ref=wide.at[group, span],
                send_sem=zsend.at[step - 1, piece],
                recv_sem=zrecv.at[step - 1, piece],
                device_id={"seq": lax.rem(seq + step * low, n)},
                device_id_type=MESH,
            )
            for step in range(1, heads_n)
        ]

    def sideways(piece):
        span = pl.ds(piece * height, height)
        return [
            to_head(
                step,
                wide.at[lax.rem(head + step, heads_n), span],
                tall.at[head, span],
                lambda i: ysend.at[i, piece],
                lambda i: yrecv.at[i, piece],
            )
            for step in range(1, heads_n)
        ]

    far = [across(piece) for piece in range(PIECES)]
    near = [sideways(piece) for piece in range(PIECES)]
    sent, passed = [], []

    def send_piece():
        if len(sent) < PIECES:
            sent.append(True)
            for copy in far[len(sent) - 1]:
                copy.start()

    def pass_piece():
        if len(passed) < PIECES:
            passed.append(True)
            for copy in far[len(passed) - 1]:
                copy.wait()
            for copy in near[len(passed) - 1]:
                copy.start()

    def beside(step):
        send_piece()
        if step >= 2:
            pass_piece()

    send_piece()
    id_copies = [to_head(step, ids_ref, ids_all.at[head], lambda i: isend.at[i], lambda i: irecv.at[i]) for step in range(1, heads_n)]
    for copy in id_copies:
        copy.start()
    load.wait()
    own_weight.wait()

    def merge(stream, chunk, recv, i):
        acc[stream, chunk] = acc[stream, chunk] + recv[stream, i]

    starts = halve(seq, bits, acc, recvs, send_sem, recv_sem, merge, beside)
    block = min(rows, LANES)
    for stream in range(2):
        mine = starts[stream][-1]
        for b in range(rows // block):
            span = slice(b * block, (b + 1) * block)
            count = columns_of(acc[stream, mine, rows + b : rows + b + 1, :])[:block]
            full[stream, mine, span, :] = (acc[stream, mine, span, :] / count).astype(jnp.bfloat16)
    double(seq, bits, starts, [full], gsend, grecv, beside)
    while len(passed) < PIECES:
        send_piece()
        pass_piece()
    puts = [pltpu.make_async_copy(wide.at[head], tall_ref.at[head], put_sem.at[0])]
    puts[0].start()
    out_ref[...] = full[...]
    own.wait()
    for copy in id_copies:
        copy.wait()
    ids_out_ref[...] = ids_all[...]
    for copies in near:
        for copy in copies:
            copy.wait()
    for step in range(1, heads_n):
        other = lax.rem(head + step, heads_n)
        puts.append(pltpu.make_async_copy(tall.at[other], tall_ref.at[other], put_sem.at[step]))
        puts[-1].start()
    for put in puts:
        put.wait()


def output_kernel(bits, heads_n, rows, part_ref, out_ref, *scratch):
    acc, full = scratch[:2]
    recvs = scratch[2 : 2 + bits]
    send_sem, recv_sem, gsend, grecv, hsend, hrecv, local_sem = scratch[2 + bits :]
    seq = lax.axis_index("seq")
    head = lax.axis_index("head")
    load = pltpu.make_async_copy(part_ref, acc, local_sem.at[0])
    load.start()
    greet(seq, bits, heads_n, False)
    load.wait()
    block = min(rows, LANES)

    def merge(stream, chunk, recv, i):
        mine = acc[stream, chunk, rows : rows + STAT, :]
        other = recv[stream, i, rows : rows + STAT, :]
        for b in range(rows // block):
            peak_a, peak_b = mine[b : b + 1], other[b : b + 1]
            peak = jnp.maximum(peak_a, peak_b)
            scale_a, scale_b = jnp.exp(peak_a - peak), jnp.exp(peak_b - peak)
            acc[stream, chunk, rows + b : rows + b + 1, :] = peak
            acc[stream, chunk, rows + 4 + b : rows + 5 + b, :] = (
                scale_a * mine[4 + b : 5 + b] + scale_b * other[4 + b : 5 + b]
            )
            span = slice(b * block, (b + 1) * block)
            acc[stream, chunk, span, :] = (
                acc[stream, chunk, span, :] * columns_of(scale_a)[:block]
                + recv[stream, i, span, :] * columns_of(scale_b)[:block]
            )

    starts = halve(seq, bits, acc, recvs, send_sem, recv_sem, merge)
    copies = []
    for stream in range(2):
        mine = starts[stream][-1]
        for b in range(rows // block):
            span = slice(b * block, (b + 1) * block)
            mass = columns_of(acc[stream, mine, rows + 4 + b : rows + 5 + b, :])[:block]
            full[head, stream, mine, span, :] = (acc[stream, mine, span, :] / mass).astype(jnp.bfloat16)
        part = full.at[head, stream, mine]
        for step in range(1, heads_n):
            copies.append(
                pltpu.make_async_remote_copy(
                    src_ref=part,
                    dst_ref=part,
                    send_sem=hsend.at[stream, step - 1],
                    recv_sem=hrecv.at[stream, step - 1],
                    device_id={"head": lax.rem(head + step, heads_n)},
                    device_id_type=MESH,
                )
            )
    for copy in copies:
        copy.start()
    for copy in copies:
        copy.wait()
    double(seq, bits, starts, [full.at[h] for h in range(heads_n)], gsend, grecv)
    out_ref[...] = full[...]


def attend_kernel(rows, centre_ref, key_ref, value_ref, out_ref):
    scores = lax.dot_general(
        centre_ref[0], key_ref[...], (((1,), (1,)), ((), ())), preferred_element_type=jnp.float32
    )
    scores = scores * (1.0 / HDIM**0.5)
    peak = jnp.max(scores, axis=1, keepdims=True)
    weights = jnp.exp(scores - peak).astype(jnp.bfloat16)
    mass = jnp.sum(weights.astype(jnp.float32), axis=1, keepdims=True)
    part = jnp.dot(weights, value_ref[...], preferred_element_type=jnp.float32)
    block = min(rows, LANES)
    for chunk in range(CLUSTERS // rows):
        out_ref[0, chunk, :rows, :] = part[chunk * rows : (chunk + 1) * rows]
        out_ref[0, chunk, rows:, :] = jnp.zeros((STAT, LANES), jnp.float32)
        for b in range(rows // block):
            first = chunk * rows + b * block
            for offset, stat in ((0, peak), (4, mass)):
                column = jnp.concatenate([stat[first : first + block]] * (LANES // block), axis=0)
                out_ref[0, chunk, rows + offset + b : rows + offset + b + 1, :] = columns_of(column)[:1]


def local(queries, keys, values, cluster_ids, out_weight):
    n = lax.axis_size("seq")
    heads_n = lax.axis_size("head")
    bits = n.bit_length() - 1
    token_rows = queries.shape[0]
    head_count = queries.shape[1] // HDIM
    rows = head_count * CLUSTERS // n // 2
    blocks = max(rows // LANES, 1)
    query_three = queries.reshape(token_rows, head_count, HDIM)
    labels = jnp.arange(CLUSTERS, dtype=jnp.int32)

    ids_t = cluster_ids.T
    member = (ids_t[:, None, :] == labels[None, :, None]).astype(jnp.bfloat16)
    totals = jnp.einsum("hct,thd->hcd", member, query_three, preferred_element_type=jnp.float32)
    counts = jnp.sum(member, axis=2, dtype=jnp.float32)

    def lanes(stat):
        stat = stat.reshape(2, n, blocks, rows // blocks)
        return jnp.pad(stat, ((0, 0), (0, 0), (0, 0), (0, LANES - rows // blocks)))

    def stats(arrays):
        each = STAT // len(arrays)
        return jnp.concatenate(
            [jnp.pad(lanes(a), ((0, 0), (0, 0), (0, each - blocks), (0, 0))) for a in arrays], axis=2
        )

    def packed(big, arrays):
        return jnp.concatenate([big.reshape(2, n, rows, HDIM), stats(arrays)], axis=2)

    vmem = pl.BlockSpec(memory_space=pltpu.VMEM)
    anywhere = pl.BlockSpec(memory_space=pl.ANY)
    dma = pltpu.SemaphoreType.DMA
    recvs = [pltpu.VMEM((2, n >> (bit + 1), rows + STAT, LANES), jnp.float32) for bit in range(bits)]
    others = max(heads_n - 1, 1)
    centre, ids_every, tall = pl.pallas_call(
        functools.partial(centre_kernel, bits, heads_n, rows),
        out_shape=(
            jax.ShapeDtypeStruct((2, n, rows, HDIM), jnp.bfloat16),
            jax.ShapeDtypeStruct((heads_n, head_count, token_rows), jnp.int32),
            jax.ShapeDtypeStruct((heads_n, *out_weight.shape), jnp.bfloat16),
        ),
        in_specs=[anywhere, vmem, anywhere],
        out_specs=(vmem, vmem, anywhere),
        scratch_shapes=[
            pltpu.VMEM((2, n, rows + STAT, LANES), jnp.float32),
            pltpu.VMEM((heads_n, head_count, token_rows), jnp.int32),
            pltpu.VMEM((2, n, rows, HDIM), jnp.bfloat16),
            pltpu.VMEM((heads_n, *out_weight.shape), jnp.bfloat16),
            pltpu.VMEM((heads_n, *out_weight.shape), jnp.bfloat16),
            *recvs,
            dma((2, bits)), dma((2, bits)), dma((2, bits, 1)), dma((2, bits, 1)),
            dma((others,)), dma((others,)), *[dma((others, PIECES)) for _ in range(4)],
            dma((3,)), dma((heads_n,)),
        ],
        compiler_params=pltpu.CompilerParams(collective_id=0, has_side_effects=True),
    )(packed(totals, [counts]), ids_t, out_weight)
    low = n // heads_n
    column_weight = lax.all_gather(
        tall.reshape(-1, out_weight.shape[1]), "seq", axis=1, tiled=True,
        axis_index_groups=[[g * low + r for r in range(low)] for g in range(heads_n)],
    )
    centre = centre.reshape(head_count, CLUSTERS, HDIM)

    chunks = CLUSTERS // rows
    parts = pl.pallas_call(
        functools.partial(attend_kernel, rows),
        out_shape=jax.ShapeDtypeStruct((head_count, chunks, rows + STAT, HDIM), jnp.float32),
        grid=(head_count,),
        in_specs=[
            pl.BlockSpec((1, CLUSTERS, HDIM), lambda h: (h, 0, 0)),
            pl.BlockSpec((token_rows, HDIM), lambda h: (0, h)),
            pl.BlockSpec((token_rows, HDIM), lambda h: (0, h)),
        ],
        out_specs=pl.BlockSpec((1, chunks, rows + STAT, HDIM), lambda h: (h, 0, 0, 0)),
        cost_estimate=pl.CostEstimate(
            flops=4 * head_count * CLUSTERS * token_rows * HDIM,
            bytes_accessed=4 * head_count * token_rows * HDIM,
            transcendentals=head_count * CLUSTERS * token_rows,
        ),
    )(centre, keys, values).reshape(2, n, rows + STAT, HDIM)

    centre_every = pl.pallas_call(
        functools.partial(output_kernel, bits, heads_n, rows),
        out_shape=jax.ShapeDtypeStruct((heads_n, 2, n, rows, HDIM), jnp.bfloat16),
        in_specs=[anywhere],
        out_specs=vmem,
        scratch_shapes=[
            pltpu.VMEM((2, n, rows + STAT, LANES), jnp.float32),
            pltpu.VMEM((heads_n, 2, n, rows, HDIM), jnp.bfloat16),
            *recvs,
            dma((2, bits)), dma((2, bits)), dma((2, bits, heads_n)), dma((2, bits, heads_n)),
            dma((2, others)), dma((2, others)), dma((1,)),
        ],
        compiler_params=pltpu.CompilerParams(collective_id=1, has_side_effects=True),
    )(parts)
    centre_every = centre_every.reshape(heads_n * head_count, CLUSTERS, HDIM)

    ids_every = ids_every.reshape(heads_n * head_count, token_rows)
    member_every = (ids_every[:, None, :] == labels[None, :, None]).astype(jnp.bfloat16)
    attended_all = jnp.einsum(
        "hct,hcd->thd", member_every, centre_every, preferred_element_type=jnp.float32
    )
    attended_all = attended_all.astype(jnp.bfloat16).reshape(token_rows, -1)
    group_rows = attended_all.shape[1] // heads_n
    summed = jnp.zeros((token_rows, column_weight.shape[1]), jnp.float32)
    for group in range(heads_n):
        term = jnp.dot(
            attended_all[:, group * group_rows : (group + 1) * group_rows],
            column_weight[group * group_rows : (group + 1) * group_rows, :],
            preferred_element_type=jnp.float32,
        )
        summed = summed + term.astype(jnp.bfloat16).astype(jnp.float32)
    return summed.astype(jnp.bfloat16)


def solution(mesh):
    return jax.shard_map(
        local,
        mesh=mesh,
        in_specs=(
            P("seq", "head"),
            P("seq", "head"),
            P("seq", "head"),
            P("seq", "head"),
            P("head", "seq"),
        ),
        out_specs=P("seq", "head"),
        check_vma=False,
    )
```

```python
import functools

import jax
import jax.numpy as jnp
from jax import lax
from jax.experimental import pallas as pl
from jax.experimental.pallas import tpu as pltpu
from jax.sharding import PartitionSpec as P

HDIM = 128
CLUSTERS = 256
LANES = 128
STAT = 8
PIECES = 4
MESH = pl.DeviceIdType.MESH


def columns_of(row):
    return jnp.broadcast_to(row, (LANES, LANES)).T


def flip(seq, bit):
    digit = lax.rem(seq // (1 << bit), 2)
    return digit, seq + (1 << bit) * (1 - 2 * digit)


def orders_of(bits):
    straight = list(range(bits))
    return [straight, straight[:1] + straight[2:] + straight[1:2]]


def greet(seq, bits, heads_n, digits):
    barrier = pltpu.get_barrier_semaphore()
    head = lax.axis_index("head")
    n = 1 << bits
    targets = [{"seq": flip(seq, bit)[1]} for bit in range(bits)]
    targets += [{"head": lax.rem(head + step, heads_n)} for step in range(1, heads_n)]
    if digits:
        low = n // heads_n
        targets += [{"seq": lax.rem(seq + step * low, n)} for step in range(1, heads_n)]
    for target in targets:
        pl.semaphore_signal(barrier, inc=1, device_id=target, device_id_type=MESH)
    pl.semaphore_wait(barrier, len(targets))


def halve(seq, bits, make, merge, beside=None):
    n = 1 << bits
    orders = orders_of(bits)
    starts = [[jnp.int32(0)] for _ in orders]

    def begin(stream, step):
        half = n >> (step + 1)
        digit, partner = flip(seq, orders[stream][step])
        start = starts[stream][step]
        give = start + (1 - digit) * half
        starts[stream].append(start + digit * half)
        copies = make(stream, step, give, half, partner)
        for copy in copies:
            copy.start()
        return copies

    pending = [begin(stream, 0) for stream in range(len(orders))]
    for step in range(bits):
        for stream in range(len(orders)):
            for copy in pending[stream]:
                copy.wait()
            keep = starts[stream][step + 1]

            def body(i, carry, stream=stream, keep=keep, step=step):
                merge(stream, step, keep + i, i)
                return carry

            lax.fori_loop(0, n >> (step + 1), body, 0)
            if step + 1 < bits:
                pending[stream] = begin(stream, step + 1)
        if beside is not None:
            beside(step)
    return starts


def double(seq, bits, starts, views, send_sem, recv_sem, beside=None):
    n = 1 << bits
    orders = orders_of(bits)

    def begin(stream, step):
        _, partner = flip(seq, orders[stream][step])
        copies = []
        for number, view in enumerate(views):
            part = view.at[stream, pl.ds(starts[stream][step + 1], n >> (step + 1))]
            copies.append(
                pltpu.make_async_remote_copy(
                    src_ref=part,
                    dst_ref=part,
                    send_sem=send_sem.at[stream, step, number],
                    recv_sem=recv_sem.at[stream, step, number],
                    device_id={"seq": partner},
                    device_id_type=MESH,
                )
            )
        for copy in copies:
            copy.start()
        return copies

    pending = [begin(stream, bits - 1) for stream in range(len(orders))]
    for step in range(bits - 1, -1, -1):
        for stream in range(len(orders)):
            for copy in pending[stream]:
                copy.wait()
            if step > 0:
                pending[stream] = begin(stream, step - 1)
        if beside is not None and step > 0:
            beside(2 * bits - 1 - step)


def centre_kernel(
    bits, heads_n, rows, part_ref, ids_ref, weight_ref, out_ref, ids_out_ref, *refs
):
    tall_refs, scratch = refs[:heads_n], refs[heads_n:]
    acc, ids_all, full, wide, tall = scratch[:5]
    recvs = scratch[5 : 5 + bits]
    send_sem, recv_sem, gsend, grecv, isend, irecv, zsend, zrecv, ysend, yrecv, local_sem = scratch[5 + bits :]
    seq = lax.axis_index("seq")
    head = lax.axis_index("head")
    n = 1 << bits
    low = n // heads_n
    group = seq // low
    load = pltpu.make_async_copy(part_ref, acc, local_sem.at[0])
    load.start()
    own = pltpu.make_async_copy(ids_ref, ids_all.at[head], local_sem.at[1])
    own.start()
    own_weight = pltpu.make_async_copy(weight_ref, wide.at[group], local_sem.at[2])
    own_weight.start()
    greet(seq, bits, heads_n, True)

    def to_head(step, src, dst, sends, receives):
        return pltpu.make_async_remote_copy(
            src_ref=src,
            dst_ref=dst,
            send_sem=sends(step - 1),
            recv_sem=receives(step - 1),
            device_id={"head": lax.rem(head + step, heads_n)},
            device_id_type=MESH,
        )

    height = weight_ref.shape[0] // PIECES

    def across(piece):
        span = pl.ds(piece * height, height)
        return [
            pltpu.make_async_remote_copy(
                src_ref=weight_ref.at[span],
                dst_ref=wide.at[group, span],
                send_sem=zsend.at[step - 1, piece],
                recv_sem=zrecv.at[step - 1, piece],
                device_id={"seq": lax.rem(seq + step * low, n)},
                device_id_type=MESH,
            )
            for step in range(1, heads_n)
        ]

    def sideways(piece):
        span = pl.ds(piece * height, height)
        return [
            to_head(
                step,
                wide.at[lax.rem(head + step, heads_n), span],
                tall.at[head, span],
                lambda i: ysend.at[i, piece],
                lambda i: yrecv.at[i, piece],
            )
            for step in range(1, heads_n)
        ]

    far = [across(piece) for piece in range(PIECES)]
    near = [sideways(piece) for piece in range(PIECES)]
    sent, passed = [], []

    def send_piece():
        if len(sent) < PIECES:
            sent.append(True)
            for copy in far[len(sent) - 1]:
                copy.start()

    def pass_piece():
        if len(passed) < PIECES:
            passed.append(True)
            for copy in far[len(passed) - 1]:
                copy.wait()
            for copy in near[len(passed) - 1]:
                copy.start()

    def beside(step):
        send_piece()
        if step >= 2:
            pass_piece()

    send_piece()
    id_copies = [to_head(step, ids_ref, ids_all.at[head], lambda i: isend.at[i], lambda i: irecv.at[i]) for step in range(1, heads_n)]
    for copy in id_copies:
        copy.start()
    load.wait()
    own_weight.wait()

    def make(stream, step, give, half, partner):
        return [
            pltpu.make_async_remote_copy(
                src_ref=acc.at[stream, pl.ds(give, half)],
                dst_ref=recvs[step].at[stream],
                send_sem=send_sem.at[stream, step],
                recv_sem=recv_sem.at[stream, step],
                device_id={"seq": partner},
                device_id_type=MESH,
            )
        ]

    def merge(stream, step, chunk, i):
        acc[stream, chunk] = acc[stream, chunk] + recvs[step][stream, i]

    starts = halve(seq, bits, make, merge, beside)
    block = min(rows, LANES)
    for stream in range(2):
        mine = starts[stream][-1]
        for b in range(rows // block):
            span = slice(b * block, (b + 1) * block)
            count = columns_of(acc[stream, mine, rows + b : rows + b + 1, :])[:block]
            full[stream, mine, span, :] = (acc[stream, mine, span, :] / count).astype(jnp.bfloat16)
    double(seq, bits, starts, [full], gsend, grecv, beside)
    while len(passed) < PIECES:
        send_piece()
        pass_piece()
    out_ref[...] = full[...]
    own.wait()
    for copy in id_copies:
        copy.wait()
    ids_out_ref[...] = ids_all[...]
    for copies in near:
        for copy in copies:
            copy.wait()
    for index, ref in enumerate(tall_refs):

        @pl.when(head == index)
        def _(index=index, ref=ref):
            ref[...] = wide[index]

        @pl.when(head != index)
        def _(index=index, ref=ref):
            ref[...] = tall[index]


def output_kernel(bits, heads_n, rows, part_ref, out_ref, *scratch):
    acc, full = scratch[:2]
    outs = scratch[2 : 2 + bits]
    recvs = scratch[2 + bits : 2 + 2 * bits]
    stat_recvs = scratch[2 + 2 * bits : 2 + 3 * bits]
    send_sem, recv_sem, gsend, grecv, hsend, hrecv, local_sem = scratch[2 + 3 * bits :]
    seq = lax.axis_index("seq")
    head = lax.axis_index("head")
    load = pltpu.make_async_copy(part_ref, acc, local_sem.at[0])
    load.start()
    greet(seq, bits, heads_n, False)
    load.wait()
    block = min(rows, LANES)

    def make(stream, step, give, half, partner):
        def convert(i, carry):
            outs[step][stream, i] = acc[stream, give + i, :rows, :].astype(jnp.bfloat16)
            return carry

        lax.fori_loop(0, half, convert, 0)
        return [
            pltpu.make_async_remote_copy(
                src_ref=src,
                dst_ref=dst,
                send_sem=send_sem.at[stream, step, number],
                recv_sem=recv_sem.at[stream, step, number],
                device_id={"seq": partner},
                device_id_type=MESH,
            )
            for number, (src, dst) in enumerate(
                (
                    (acc.at[stream, pl.ds(give, half), pl.ds(rows, STAT)], stat_recvs[step].at[stream]),
                    (outs[step].at[stream], recvs[step].at[stream]),
                )
            )
        ]

    def merge(stream, step, chunk, i):
        mine = acc[stream, chunk, rows : rows + STAT, :]
        other = stat_recvs[step][stream, i]
        for b in range(rows // block):
            peak_a, peak_b = mine[b : b + 1], other[b : b + 1]
            peak = jnp.maximum(peak_a, peak_b)
            scale_a, scale_b = jnp.exp(peak_a - peak), jnp.exp(peak_b - peak)
            acc[stream, chunk, rows + b : rows + b + 1, :] = peak
            acc[stream, chunk, rows + 4 + b : rows + 5 + b, :] = (
                scale_a * mine[4 + b : 5 + b] + scale_b * other[4 + b : 5 + b]
            )
            span = slice(b * block, (b + 1) * block)
            acc[stream, chunk, span, :] = (
                acc[stream, chunk, span, :] * columns_of(scale_a)[:block]
                + recvs[step][stream, i, span, :].astype(jnp.float32) * columns_of(scale_b)[:block]
            )

    starts = halve(seq, bits, make, merge)
    copies = []
    for stream in range(2):
        mine = starts[stream][-1]
        for b in range(rows // block):
            span = slice(b * block, (b + 1) * block)
            mass = columns_of(acc[stream, mine, rows + 4 + b : rows + 5 + b, :])[:block]
            full[head, stream, mine, span, :] = (acc[stream, mine, span, :] / mass).astype(jnp.bfloat16)
        part = full.at[head, stream, mine]
        for step in range(1, heads_n):
            copies.append(
                pltpu.make_async_remote_copy(
                    src_ref=part,
                    dst_ref=part,
                    send_sem=hsend.at[stream, step - 1],
                    recv_sem=hrecv.at[stream, step - 1],
                    device_id={"head": lax.rem(head + step, heads_n)},
                    device_id_type=MESH,
                )
            )
    for copy in copies:
        copy.start()
    for copy in copies:
        copy.wait()
    double(seq, bits, starts, [full.at[h] for h in range(heads_n)], gsend, grecv)
    out_ref[...] = full[...]


def attend_kernel(rows, centre_ref, key_ref, value_ref, out_ref):
    scores = lax.dot_general(
        centre_ref[0], key_ref[...], (((1,), (1,)), ((), ())), preferred_element_type=jnp.float32
    )
    scores = scores * (1.0 / HDIM**0.5)
    peak = jnp.max(scores, axis=1, keepdims=True)
    weights = jnp.exp(scores - peak).astype(jnp.bfloat16)
    mass = jnp.sum(weights.astype(jnp.float32), axis=1, keepdims=True)
    part = jnp.dot(weights, value_ref[...], preferred_element_type=jnp.float32)
    block = min(rows, LANES)
    for chunk in range(CLUSTERS // rows):
        out_ref[0, chunk, :rows, :] = part[chunk * rows : (chunk + 1) * rows]
        out_ref[0, chunk, rows:, :] = jnp.zeros((STAT, LANES), jnp.float32)
        for b in range(rows // block):
            first = chunk * rows + b * block
            for offset, stat in ((0, peak), (4, mass)):
                column = jnp.concatenate([stat[first : first + block]] * (LANES // block), axis=0)
                out_ref[0, chunk, rows + offset + b : rows + offset + b + 1, :] = columns_of(column)[:1]


def local(queries, keys, values, cluster_ids, out_weight):
    n = lax.axis_size("seq")
    heads_n = lax.axis_size("head")
    bits = n.bit_length() - 1
    token_rows = queries.shape[0]
    head_count = queries.shape[1] // HDIM
    rows = head_count * CLUSTERS // n // 2
    blocks = max(rows // LANES, 1)
    query_three = queries.reshape(token_rows, head_count, HDIM)
    labels = jnp.arange(CLUSTERS, dtype=jnp.int32)

    ids_t = cluster_ids.T
    member = (ids_t[:, None, :] == labels[None, :, None]).astype(jnp.bfloat16)
    totals = jnp.einsum("hct,thd->hcd", member, query_three, preferred_element_type=jnp.float32)
    counts = jnp.sum(member, axis=2, dtype=jnp.float32)

    def lanes(stat):
        stat = stat.reshape(2, n, blocks, rows // blocks)
        return jnp.pad(stat, ((0, 0), (0, 0), (0, 0), (0, LANES - rows // blocks)))

    def stats(arrays):
        each = STAT // len(arrays)
        return jnp.concatenate(
            [jnp.pad(lanes(a), ((0, 0), (0, 0), (0, each - blocks), (0, 0))) for a in arrays], axis=2
        )

    def packed(big, arrays):
        return jnp.concatenate([big.reshape(2, n, rows, HDIM), stats(arrays)], axis=2)

    vmem = pl.BlockSpec(memory_space=pltpu.VMEM)
    anywhere = pl.BlockSpec(memory_space=pl.ANY)
    dma = pltpu.SemaphoreType.DMA
    recvs = [pltpu.VMEM((2, n >> (bit + 1), rows + STAT, LANES), jnp.float32) for bit in range(bits)]
    others = max(heads_n - 1, 1)
    centre, ids_every, *tall = pl.pallas_call(
        functools.partial(centre_kernel, bits, heads_n, rows),
        out_shape=(
            jax.ShapeDtypeStruct((2, n, rows, HDIM), jnp.bfloat16),
            jax.ShapeDtypeStruct((heads_n, head_count, token_rows), jnp.int32),
            *[jax.ShapeDtypeStruct(out_weight.shape, jnp.bfloat16) for _ in range(heads_n)],
        ),
        in_specs=[anywhere, vmem, anywhere],
        out_specs=(vmem, vmem, *[vmem] * heads_n),
        scratch_shapes=[
            pltpu.VMEM((2, n, rows + STAT, LANES), jnp.float32),
            pltpu.VMEM((heads_n, head_count, token_rows), jnp.int32),
            pltpu.VMEM((2, n, rows, HDIM), jnp.bfloat16),
            pltpu.VMEM((heads_n, *out_weight.shape), jnp.bfloat16),
            pltpu.VMEM((heads_n, *out_weight.shape), jnp.bfloat16),
            *recvs,
            dma((2, bits)), dma((2, bits)), dma((2, bits, 1)), dma((2, bits, 1)),
            dma((others,)), dma((others,)), *[dma((others, PIECES)) for _ in range(4)],
            dma((3,)),
        ],
        compiler_params=pltpu.CompilerParams(collective_id=0, has_side_effects=True),
    )(packed(totals, [counts]), ids_t, out_weight)
    low = n // heads_n
    groups = [[g * low + r for r in range(low)] for g in range(heads_n)]
    column_weight = [
        lax.all_gather(tall[group], "seq", axis=1, tiled=True, axis_index_groups=groups)
        for group in range(heads_n)
    ]
    centre = centre.reshape(head_count, CLUSTERS, HDIM)

    chunks = CLUSTERS // rows
    parts = pl.pallas_call(
        functools.partial(attend_kernel, rows),
        out_shape=jax.ShapeDtypeStruct((head_count, chunks, rows + STAT, HDIM), jnp.float32),
        grid=(head_count,),
        in_specs=[
            pl.BlockSpec((1, CLUSTERS, HDIM), lambda h: (h, 0, 0)),
            pl.BlockSpec((token_rows, HDIM), lambda h: (0, h)),
            pl.BlockSpec((token_rows, HDIM), lambda h: (0, h)),
        ],
        out_specs=pl.BlockSpec((1, chunks, rows + STAT, HDIM), lambda h: (h, 0, 0, 0)),
        cost_estimate=pl.CostEstimate(
            flops=4 * head_count * CLUSTERS * token_rows * HDIM,
            bytes_accessed=4 * head_count * token_rows * HDIM,
            transcendentals=head_count * CLUSTERS * token_rows,
        ),
    )(centre, keys, values).reshape(2, n, rows + STAT, HDIM)

    centre_every = pl.pallas_call(
        functools.partial(output_kernel, bits, heads_n, rows),
        out_shape=jax.ShapeDtypeStruct((heads_n, 2, n, rows, HDIM), jnp.bfloat16),
        in_specs=[anywhere],
        out_specs=vmem,
        scratch_shapes=[
            pltpu.VMEM((2, n, rows + STAT, LANES), jnp.float32),
            pltpu.VMEM((heads_n, 2, n, rows, HDIM), jnp.bfloat16),
            *[pltpu.VMEM((2, n >> (bit + 1), rows, LANES), jnp.bfloat16) for _ in range(2) for bit in range(bits)],
            *[pltpu.VMEM((2, n >> (bit + 1), STAT, LANES), jnp.float32) for bit in range(bits)],
            dma((2, bits, 2)), dma((2, bits, 2)), dma((2, bits, heads_n)), dma((2, bits, heads_n)),
            dma((2, others)), dma((2, others)), dma((1,)),
        ],
        compiler_params=pltpu.CompilerParams(collective_id=1, has_side_effects=True),
    )(parts)
    centre_every = centre_every.reshape(heads_n * head_count, CLUSTERS, HDIM)

    ids_every = ids_every.reshape(heads_n * head_count, token_rows)
    member_every = (ids_every[:, None, :] == labels[None, :, None]).astype(jnp.bfloat16)
    attended_all = jnp.einsum(
        "hct,hcd->thd", member_every, centre_every, preferred_element_type=jnp.float32
    )
    attended_all = attended_all.astype(jnp.bfloat16).reshape(token_rows, -1)
    group_rows = attended_all.shape[1] // heads_n
    summed = jnp.zeros((token_rows, column_weight[0].shape[1]), jnp.float32)
    for group in range(heads_n):
        term = jnp.dot(
            attended_all[:, group * group_rows : (group + 1) * group_rows],
            column_weight[group],
            preferred_element_type=jnp.float32,
        )
        summed = summed + term.astype(jnp.bfloat16).astype(jnp.float32)
    return summed.astype(jnp.bfloat16)


def solution(mesh):
    return jax.shard_map(
        local,
        mesh=mesh,
        in_specs=(
            P("seq", "head"),
            P("seq", "head"),
            P("seq", "head"),
            P("seq", "head"),
            P("head", "seq"),
        ),
        out_specs=P("seq", "head"),
        check_vma=False,
    )
```

```python
import functools

import jax
import jax.numpy as jnp
from jax import lax
from jax.experimental import pallas as pl
from jax.experimental.pallas import tpu as pltpu
from jax.sharding import PartitionSpec as P

HDIM = 128
CLUSTERS = 256
LANES = 128
STAT = 8
PIECES = 4
MESH = pl.DeviceIdType.MESH


def columns_of(row):
    return jnp.broadcast_to(row, (LANES, LANES)).T


def flip(seq, bit):
    digit = lax.rem(seq // (1 << bit), 2)
    return digit, seq + (1 << bit) * (1 - 2 * digit)


def orders_of(bits):
    straight = list(range(bits))
    return [straight, straight[:1] + straight[2:] + straight[1:2]]


def greet(seq, bits, heads_n, digits):
    barrier = pltpu.get_barrier_semaphore()
    head = lax.axis_index("head")
    n = 1 << bits
    targets = [{"seq": flip(seq, bit)[1]} for bit in range(bits)]
    targets += [{"head": lax.rem(head + step, heads_n)} for step in range(1, heads_n)]
    if digits:
        low = n // heads_n
        targets += [{"seq": lax.rem(seq + step * low, n)} for step in range(1, heads_n)]
    for target in targets:
        pl.semaphore_signal(barrier, inc=1, device_id=target, device_id_type=MESH)
    pl.semaphore_wait(barrier, len(targets))


def halve(seq, bits, make, merge, beside=None):
    n = 1 << bits
    orders = orders_of(bits)
    starts = [[jnp.int32(0)] for _ in orders]

    def begin(stream, step):
        half = n >> (step + 1)
        digit, partner = flip(seq, orders[stream][step])
        start = starts[stream][step]
        give = start + (1 - digit) * half
        starts[stream].append(start + digit * half)
        copies = make(stream, step, give, half, partner)
        for copy in copies:
            copy.start()
        return copies

    pending = [begin(stream, 0) for stream in range(len(orders))]
    for step in range(bits):
        for stream in range(len(orders)):
            for copy in pending[stream]:
                copy.wait()
            keep = starts[stream][step + 1]

            def body(i, carry, stream=stream, keep=keep, step=step):
                merge(stream, step, keep + i, i)
                return carry

            lax.fori_loop(0, n >> (step + 1), body, 0)
            if step + 1 < bits:
                pending[stream] = begin(stream, step + 1)
        if beside is not None:
            beside(step)
    return starts


def double(seq, bits, starts, views, send_sem, recv_sem, beside=None):
    n = 1 << bits
    orders = orders_of(bits)

    def begin(stream, step):
        _, partner = flip(seq, orders[stream][step])
        copies = []
        for number, view in enumerate(views):
            part = view.at[stream, pl.ds(starts[stream][step + 1], n >> (step + 1))]
            copies.append(
                pltpu.make_async_remote_copy(
                    src_ref=part,
                    dst_ref=part,
                    send_sem=send_sem.at[stream, step, number],
                    recv_sem=recv_sem.at[stream, step, number],
                    device_id={"seq": partner},
                    device_id_type=MESH,
                )
            )
        for copy in copies:
            copy.start()
        return copies

    pending = [begin(stream, bits - 1) for stream in range(len(orders))]
    for step in range(bits - 1, -1, -1):
        for stream in range(len(orders)):
            for copy in pending[stream]:
                copy.wait()
            if step > 0:
                pending[stream] = begin(stream, step - 1)
        if beside is not None and step > 0:
            beside(2 * bits - 1 - step)


def centre_kernel(
    bits, heads_n, rows, part_ref, ids_ref, weight_ref, out_ref, ids_out_ref, *refs
):
    tall_refs, scratch = refs[:heads_n], refs[heads_n:]
    acc, ids_all, full, wide, tall = scratch[:5]
    recvs = scratch[5 : 5 + bits]
    send_sem, recv_sem, gsend, grecv, isend, irecv, zsend, zrecv, ysend, yrecv, local_sem = scratch[5 + bits :]
    seq = lax.axis_index("seq")
    head = lax.axis_index("head")
    n = 1 << bits
    low = n // heads_n
    group = seq // low
    load = pltpu.make_async_copy(part_ref, acc, local_sem.at[0])
    load.start()
    own = pltpu.make_async_copy(ids_ref, ids_all.at[head], local_sem.at[1])
    own.start()
    own_weight = pltpu.make_async_copy(weight_ref, wide.at[group], local_sem.at[2])
    own_weight.start()
    greet(seq, bits, heads_n, True)

    def to_head(step, src, dst, sends, receives):
        return pltpu.make_async_remote_copy(
            src_ref=src,
            dst_ref=dst,
            send_sem=sends(step - 1),
            recv_sem=receives(step - 1),
            device_id={"head": lax.rem(head + step, heads_n)},
            device_id_type=MESH,
        )

    height = weight_ref.shape[0] // PIECES

    def across(piece):
        span = pl.ds(piece * height, height)
        return [
            pltpu.make_async_remote_copy(
                src_ref=weight_ref.at[span],
                dst_ref=wide.at[group, span],
                send_sem=zsend.at[step - 1, piece],
                recv_sem=zrecv.at[step - 1, piece],
                device_id={"seq": lax.rem(seq + step * low, n)},
                device_id_type=MESH,
            )
            for step in range(1, heads_n)
        ]

    def sideways(piece):
        span = pl.ds(piece * height, height)
        return [
            to_head(
                step,
                wide.at[lax.rem(head + step, heads_n), span],
                tall.at[head, span],
                lambda i: ysend.at[i, piece],
                lambda i: yrecv.at[i, piece],
            )
            for step in range(1, heads_n)
        ]

    far = [across(piece) for piece in range(PIECES)]
    near = [sideways(piece) for piece in range(PIECES)]
    sent, passed = [], []

    def send_piece():
        if len(sent) < PIECES:
            sent.append(True)
            for copy in far[len(sent) - 1]:
                copy.start()

    def pass_piece():
        if len(passed) < PIECES:
            passed.append(True)
            for copy in far[len(passed) - 1]:
                copy.wait()
            for copy in near[len(passed) - 1]:
                copy.start()

    def beside(step):
        send_piece()
        if step >= 1:
            pass_piece()

    send_piece()
    send_piece()
    id_copies = [to_head(step, ids_ref, ids_all.at[head], lambda i: isend.at[i], lambda i: irecv.at[i]) for step in range(1, heads_n)]
    for copy in id_copies:
        copy.start()
    load.wait()
    own_weight.wait()

    def make(stream, step, give, half, partner):
        return [
            pltpu.make_async_remote_copy(
                src_ref=acc.at[stream, pl.ds(give, half)],
                dst_ref=recvs[step].at[stream],
                send_sem=send_sem.at[stream, step],
                recv_sem=recv_sem.at[stream, step],
                device_id={"seq": partner},
                device_id_type=MESH,
            )
        ]

    def merge(stream, step, chunk, i):
        acc[stream, chunk] = acc[stream, chunk] + recvs[step][stream, i]

    starts = halve(seq, bits, make, merge, beside)
    block = min(rows, LANES)
    for stream in range(2):
        mine = starts[stream][-1]
        for b in range(rows // block):
            span = slice(b * block, (b + 1) * block)
            count = columns_of(acc[stream, mine, rows + b : rows + b + 1, :])[:block]
            full[stream, mine, span, :] = (acc[stream, mine, span, :] / count).astype(jnp.bfloat16)
    double(seq, bits, starts, [full], gsend, grecv, beside)
    while len(passed) < PIECES:
        send_piece()
        pass_piece()
    out_ref[...] = full[...]
    own.wait()
    for copy in id_copies:
        copy.wait()
    ids_out_ref[...] = ids_all[...]
    for copies in near:
        for copy in copies:
            copy.wait()
    for index, ref in enumerate(tall_refs):

        @pl.when(head == index)
        def _(index=index, ref=ref):
            ref[...] = wide[index]

        @pl.when(head != index)
        def _(index=index, ref=ref):
            ref[...] = tall[index]


def output_kernel(bits, heads_n, rows, part_ref, out_ref, *scratch):
    acc, full = scratch[:2]
    outs = scratch[2 : 2 + bits]
    recvs = scratch[2 + bits : 2 + 2 * bits]
    stat_recvs = scratch[2 + 2 * bits : 2 + 3 * bits]
    send_sem, recv_sem, gsend, grecv, hsend, hrecv, local_sem = scratch[2 + 3 * bits :]
    seq = lax.axis_index("seq")
    head = lax.axis_index("head")
    load = pltpu.make_async_copy(part_ref, acc, local_sem.at[0])
    load.start()
    greet(seq, bits, heads_n, False)
    load.wait()
    block = min(rows, LANES)

    def make(stream, step, give, half, partner):
        def convert(i, carry):
            outs[step][stream, i] = acc[stream, give + i, :rows, :].astype(jnp.bfloat16)
            return carry

        lax.fori_loop(0, half, convert, 0)
        return [
            pltpu.make_async_remote_copy(
                src_ref=src,
                dst_ref=dst,
                send_sem=send_sem.at[stream, step, number],
                recv_sem=recv_sem.at[stream, step, number],
                device_id={"seq": partner},
                device_id_type=MESH,
            )
            for number, (src, dst) in enumerate(
                (
                    (acc.at[stream, pl.ds(give, half), pl.ds(rows, STAT)], stat_recvs[step].at[stream]),
                    (outs[step].at[stream], recvs[step].at[stream]),
                )
            )
        ]

    def merge(stream, step, chunk, i):
        mine = acc[stream, chunk, rows : rows + STAT, :]
        other = stat_recvs[step][stream, i]
        for b in range(rows // block):
            peak_a, peak_b = mine[b : b + 1], other[b : b + 1]
            peak = jnp.maximum(peak_a, peak_b)
            scale_a, scale_b = jnp.exp(peak_a - peak), jnp.exp(peak_b - peak)
            acc[stream, chunk, rows + b : rows + b + 1, :] = peak
            acc[stream, chunk, rows + 4 + b : rows + 5 + b, :] = (
                scale_a * mine[4 + b : 5 + b] + scale_b * other[4 + b : 5 + b]
            )
            span = slice(b * block, (b + 1) * block)
            acc[stream, chunk, span, :] = (
                acc[stream, chunk, span, :] * columns_of(scale_a)[:block]
                + recvs[step][stream, i, span, :].astype(jnp.float32) * columns_of(scale_b)[:block]
            )

    starts = halve(seq, bits, make, merge)
    copies = []
    for stream in range(2):
        mine = starts[stream][-1]
        for b in range(rows // block):
            span = slice(b * block, (b + 1) * block)
            mass = columns_of(acc[stream, mine, rows + 4 + b : rows + 5 + b, :])[:block]
            full[head, stream, mine, span, :] = (acc[stream, mine, span, :] / mass).astype(jnp.bfloat16)
        part = full.at[head, stream, mine]
        for step in range(1, heads_n):
            copies.append(
                pltpu.make_async_remote_copy(
                    src_ref=part,
                    dst_ref=part,
                    send_sem=hsend.at[stream, step - 1],
                    recv_sem=hrecv.at[stream, step - 1],
                    device_id={"head": lax.rem(head + step, heads_n)},
                    device_id_type=MESH,
                )
            )
    for copy in copies:
        copy.start()
    for copy in copies:
        copy.wait()
    double(seq, bits, starts, [full.at[h] for h in range(heads_n)], gsend, grecv)
    out_ref[...] = full[...]


def attend_kernel(rows, centre_ref, key_ref, value_ref, out_ref):
    scores = lax.dot_general(
        centre_ref[0], key_ref[...], (((1,), (1,)), ((), ())), preferred_element_type=jnp.float32
    )
    scores = scores * (1.0 / HDIM**0.5)
    peak = jnp.max(scores, axis=1, keepdims=True)
    weights = jnp.exp(scores - peak).astype(jnp.bfloat16)
    mass = jnp.sum(weights.astype(jnp.float32), axis=1, keepdims=True)
    part = jnp.dot(weights, value_ref[...], preferred_element_type=jnp.float32)
    block = min(rows, LANES)
    for chunk in range(CLUSTERS // rows):
        out_ref[0, chunk, :rows, :] = part[chunk * rows : (chunk + 1) * rows]
        out_ref[0, chunk, rows:, :] = jnp.zeros((STAT, LANES), jnp.float32)
        for b in range(rows // block):
            first = chunk * rows + b * block
            for offset, stat in ((0, peak), (4, mass)):
                column = jnp.concatenate([stat[first : first + block]] * (LANES // block), axis=0)
                out_ref[0, chunk, rows + offset + b : rows + offset + b + 1, :] = columns_of(column)[:1]


def local(queries, keys, values, cluster_ids, out_weight):
    n = lax.axis_size("seq")
    heads_n = lax.axis_size("head")
    bits = n.bit_length() - 1
    token_rows = queries.shape[0]
    head_count = queries.shape[1] // HDIM
    rows = head_count * CLUSTERS // n // 2
    blocks = max(rows // LANES, 1)
    query_three = queries.reshape(token_rows, head_count, HDIM)
    labels = jnp.arange(CLUSTERS, dtype=jnp.int32)

    ids_t = cluster_ids.T
    member = (ids_t[:, None, :] == labels[None, :, None]).astype(jnp.bfloat16)
    totals = jnp.einsum("hct,thd->hcd", member, query_three, preferred_element_type=jnp.float32)
    counts = jnp.sum(member, axis=2, dtype=jnp.float32)

    def lanes(stat):
        stat = stat.reshape(2, n, blocks, rows // blocks)
        return jnp.pad(stat, ((0, 0), (0, 0), (0, 0), (0, LANES - rows // blocks)))

    def stats(arrays):
        each = STAT // len(arrays)
        return jnp.concatenate(
            [jnp.pad(lanes(a), ((0, 0), (0, 0), (0, each - blocks), (0, 0))) for a in arrays], axis=2
        )

    def packed(big, arrays):
        return jnp.concatenate([big.reshape(2, n, rows, HDIM), stats(arrays)], axis=2)

    vmem = pl.BlockSpec(memory_space=pltpu.VMEM)
    anywhere = pl.BlockSpec(memory_space=pl.ANY)
    dma = pltpu.SemaphoreType.DMA
    recvs = [pltpu.VMEM((2, n >> (bit + 1), rows + STAT, LANES), jnp.float32) for bit in range(bits)]
    others = max(heads_n - 1, 1)
    centre, ids_every, *tall = pl.pallas_call(
        functools.partial(centre_kernel, bits, heads_n, rows),
        out_shape=(
            jax.ShapeDtypeStruct((2, n, rows, HDIM), jnp.bfloat16),
            jax.ShapeDtypeStruct((heads_n, head_count, token_rows), jnp.int32),
            *[jax.ShapeDtypeStruct(out_weight.shape, jnp.bfloat16) for _ in range(heads_n)],
        ),
        in_specs=[anywhere, vmem, anywhere],
        out_specs=(vmem, vmem, *[vmem] * heads_n),
        scratch_shapes=[
            pltpu.VMEM((2, n, rows + STAT, LANES), jnp.float32),
            pltpu.VMEM((heads_n, head_count, token_rows), jnp.int32),
            pltpu.VMEM((2, n, rows, HDIM), jnp.bfloat16),
            pltpu.VMEM((heads_n, *out_weight.shape), jnp.bfloat16),
            pltpu.VMEM((heads_n, *out_weight.shape), jnp.bfloat16),
            *recvs,
            dma((2, bits)), dma((2, bits)), dma((2, bits, 1)), dma((2, bits, 1)),
            dma((others,)), dma((others,)), *[dma((others, PIECES)) for _ in range(4)],
            dma((3,)),
        ],
        compiler_params=pltpu.CompilerParams(collective_id=0, has_side_effects=True),
    )(packed(totals, [counts]), ids_t, out_weight)
    low = n // heads_n
    groups = [[g * low + r for r in range(low)] for g in range(heads_n)]
    column_weight = [
        lax.all_gather(tall[group], "seq", axis=1, tiled=True, axis_index_groups=groups)
        for group in range(heads_n)
    ]
    centre = centre.reshape(head_count, CLUSTERS, HDIM)

    chunks = CLUSTERS // rows
    parts = pl.pallas_call(
        functools.partial(attend_kernel, rows),
        out_shape=jax.ShapeDtypeStruct((head_count, chunks, rows + STAT, HDIM), jnp.float32),
        grid=(head_count,),
        in_specs=[
            pl.BlockSpec((1, CLUSTERS, HDIM), lambda h: (h, 0, 0)),
            pl.BlockSpec((token_rows, HDIM), lambda h: (0, h)),
            pl.BlockSpec((token_rows, HDIM), lambda h: (0, h)),
        ],
        out_specs=pl.BlockSpec((1, chunks, rows + STAT, HDIM), lambda h: (h, 0, 0, 0)),
        cost_estimate=pl.CostEstimate(
            flops=4 * head_count * CLUSTERS * token_rows * HDIM,
            bytes_accessed=4 * head_count * token_rows * HDIM,
            transcendentals=head_count * CLUSTERS * token_rows,
        ),
    )(centre, keys, values).reshape(2, n, rows + STAT, HDIM)

    centre_every = pl.pallas_call(
        functools.partial(output_kernel, bits, heads_n, rows),
        out_shape=jax.ShapeDtypeStruct((heads_n, 2, n, rows, HDIM), jnp.bfloat16),
        in_specs=[anywhere],
        out_specs=vmem,
        scratch_shapes=[
            pltpu.VMEM((2, n, rows + STAT, LANES), jnp.float32),
            pltpu.VMEM((heads_n, 2, n, rows, HDIM), jnp.bfloat16),
            *[pltpu.VMEM((2, n >> (bit + 1), rows, LANES), jnp.bfloat16) for _ in range(2) for bit in range(bits)],
            *[pltpu.VMEM((2, n >> (bit + 1), STAT, LANES), jnp.float32) for bit in range(bits)],
            dma((2, bits, 2)), dma((2, bits, 2)), dma((2, bits, heads_n)), dma((2, bits, heads_n)),
            dma((2, others)), dma((2, others)), dma((1,)),
        ],
        compiler_params=pltpu.CompilerParams(collective_id=1, has_side_effects=True),
    )(parts)
    centre_every = centre_every.reshape(heads_n * head_count, CLUSTERS, HDIM)

    ids_every = ids_every.reshape(heads_n * head_count, token_rows)
    member_every = (ids_every[:, None, :] == labels[None, :, None]).astype(jnp.bfloat16)
    attended_all = jnp.einsum(
        "hct,hcd->thd", member_every, centre_every, preferred_element_type=jnp.float32
    )
    attended_all = attended_all.astype(jnp.bfloat16).reshape(token_rows, -1)
    group_rows = attended_all.shape[1] // heads_n
    summed = jnp.zeros((token_rows, column_weight[0].shape[1]), jnp.float32)
    for group in range(heads_n):
        term = jnp.dot(
            attended_all[:, group * group_rows : (group + 1) * group_rows],
            column_weight[group],
            preferred_element_type=jnp.float32,
        )
        summed = summed + term.astype(jnp.bfloat16).astype(jnp.float32)
    return summed.astype(jnp.bfloat16)


def solution(mesh):
    return jax.shard_map(
        local,
        mesh=mesh,
        in_specs=(
            P("seq", "head"),
            P("seq", "head"),
            P("seq", "head"),
            P("seq", "head"),
            P("head", "seq"),
        ),
        out_specs=P("seq", "head"),
        check_vma=False,
    )
```
